32 devices in a mesh: dp: 4 (over z), row: 4 (over y, core), col: 2 (over x).
Axes of the slice: x: 2, y: 2, z: 4, core: 2. Of those that a mesh axis runs over, the one named last changes fastest.
Arguments:
- latents: bfloat16 [4096, 2048], P(('dp', 'col'), 'row'), parts along dimension 0, may hold values from -64 to 64
- norm_gain: float32 [8192], P(('dp', 'row')), parts along dimension 0, may hold values from 0.1 to 1.9
- q_weight: bfloat16 [8192, 2048], P(('dp', 'row'), 'col'), parts along dimension 0, may hold values from -1 to 1
- k_weight: bfloat16 [8192, 2048], P(('dp', 'row'), 'col'), parts along dimension 0, may hold values from -1 to 1
- v_weight: bfloat16 [8192, 2048], P(('dp', 'row'), 'col'), parts along dimension 0, may hold values from -0.125 to 0.125
- out_weight: bfloat16 [8192, 2048], P(('dp', 'col'), 'row'), parts along dimension 0, may hold values from -0.5 to 0.5
Outputs:
- attended: bfloat16 [4096, 2048], P(('dp', 'col'), 'row'), parts along dimension 0
The draws below stay inside these ranges and needn't reach their ends.
There are 4 independent parts, one for each index of `dp`. The reference program is written for one: setup_inputs(seed, part) draws one part's arguments, and reference() takes and returns one part's arrays. A program takes and returns all parts, laid end to end along the dimension named above; each array names one. Nothing has to cross between parts.
All inputs are finite; a program needn't handle non-finite values.
Results may differ from the reference program's by a relative error of at most 0.03.
Values may be sent and summed in bfloat16 or wider, within the bound.
A program may use at most 64 MiB of HBM per device.

```python
import jax
import jax.numpy as jnp
from jax import lax

HEADS = 16
HEAD_DIM = 128
D = 2048
LATENTS = 1024
N_ROW = 4
N_COL = 2


def draw_latents(key, part):
    noise = jnp.clip(jax.random.normal(jax.random.fold_in(key, 1), (LATENTS, D), jnp.float32), -6.0, 6.0)
    ramp = jnp.arange(D, dtype=jnp.float32) / D
    values = noise * (3.0 ** ramp)[None, :]
    return jnp.clip(values, -64.0, 64.0).astype(jnp.bfloat16)


def projection(key, salt):
    base = jnp.clip(jax.random.normal(jax.random.fold_in(key, salt), (D, D), jnp.float32), -6.0, 6.0)
    return base * jnp.sqrt(2.0 / D)


def draw_q_weight(key, part):
    values = projection(key, 21)
    return jnp.clip(values, -1.0, 1.0).astype(jnp.bfloat16)


def draw_k_weight(key, part):
    values = projection(key, 22)
    return jnp.clip(values, -1.0, 1.0).astype(jnp.bfloat16)


def shard_levels(key, shape, split, low, largest):
    gain = 1.0
    for position, blocks in split:
        draws = jax.random.uniform(jax.random.fold_in(jax.random.fold_in(key, 6), position), (blocks,), jnp.float32, low / len(split), largest / len(split))
        gain = gain * jnp.repeat(jnp.exp(draws), shape[position] // blocks).reshape((-1,) + (1,) * (len(shape) - 1 - position))
    return gain


def centred(own_key, shape, scale, limit, cuts=(), held_as=jnp.bfloat16):
    gain = shard_levels(own_key, shape, cuts, -0.22, 0.18) if cuts else 1.0
    result = jax.random.normal(own_key, shape, jnp.float32) * scale * gain
    return jnp.minimum(jnp.maximum(result, -limit), limit).astype(held_as)


def setup_inputs(seed: int = 0, part: int = 0) -> dict:
    key_of = jax.random.split(jax.random.key(seed), 7)
    part_splits = jax.random.split(jax.random.fold_in(key_of[6], part), 7)
    return {
        "latents": draw_latents(jax.random.fold_in(jax.random.fold_in(key_of[6], part), 71), part),
        "norm_gain": jnp.clip(1.0 + 0.18 * jax.random.normal(part_splits[1], (D,), jnp.float32), 0.1, 1.9),
        "q_weight": draw_q_weight(jax.random.fold_in(jax.random.fold_in(key_of[6], part), 71), part),
        "k_weight": draw_k_weight(jax.random.fold_in(jax.random.fold_in(key_of[6], part), 71), part),
        "v_weight": centred(part_splits[4], (D, D), D ** -0.5, 0.125, ((0, 4), (1, 2))),
        "out_weight": centred(part_splits[5], (D, D), (D // 16) ** -0.5, 0.5, ((0, 2), (1, 4))),
    }


def blocked_sum(left, weight, pieces):
    width = left.shape[1] // pieces
    acc = jnp.zeros((left.shape[0], weight.shape[1]), jnp.float32)
    for index in range(pieces):
        part = jnp.dot(left[:, index * width:(index + 1) * width].astype(jnp.float32), weight[index * width:(index + 1) * width, :].astype(jnp.float32), preferred_element_type=jnp.float32)
        part = lax.optimization_barrier(part.astype(jnp.bfloat16))
        acc = acc + part.astype(jnp.float32)
    return acc.astype(jnp.bfloat16)

def reference(latents, norm_gain, q_weight, k_weight, v_weight, out_weight):
    wide = latents.astype(jnp.float32)
    total = lax.optimization_barrier(jnp.sum(wide * wide, axis=1))
    normed = (wide * lax.rsqrt(total / D + 1e-06)[:, None] * norm_gain[None, :]).astype(jnp.bfloat16)
    query = blocked_sum(normed, q_weight, N_ROW)
    keys = blocked_sum(normed, k_weight, N_ROW)
    values = blocked_sum(normed, v_weight, N_ROW)
    query3 = query.astype(jnp.float32).reshape(LATENTS, HEADS, HEAD_DIM)
    keys3 = keys.astype(jnp.float32).reshape(LATENTS, HEADS, HEAD_DIM)
    values3 = values.astype(jnp.float32).reshape(LATENTS, HEADS, HEAD_DIM)
    scores = jnp.einsum('qhd,khd->hqk', query3, keys3) / jnp.sqrt(jnp.float32(HEAD_DIM))
    peak = lax.optimization_barrier(jnp.max(scores, axis=2, keepdims=True))
    weights = jnp.exp(scores - peak)
    denom = lax.optimization_barrier(jnp.sum(weights, axis=2))
    rounded = weights.astype(jnp.bfloat16).astype(jnp.float32)
    mixed = jnp.einsum('hqk,khd->hqd', rounded, values3) / denom[:, :, None]
    mixed = jnp.transpose(mixed, (1, 0, 2)).reshape(LATENTS, D).astype(jnp.bfloat16)
    return blocked_sum(mixed, out_weight, N_COL)
```

```python
import functools
import math

import jax
import jax.numpy as jnp
from jax import lax
from jax.experimental import pallas as pl
from jax.experimental.pallas import tpu as pltpu
from jax.sharding import PartitionSpec as P

HEAD_DIM = 128
EPS = 1e-06
MESH = pl.DeviceIdType.MESH
F32 = jnp.float32
BF16 = jnp.bfloat16
KEY, VALUE, QUERY = 0, 1, 2


def kernel(
    row_count, chunk,
    x_hbm, gain_hbm, k_hbm, v_hbm, q_hbm, o_hbm, out_ref,
    xraw, gains, wbuf, wo, xg, ssq, ssq_out, ssq_in, scale, psend, precv, pown,
    qkv, mix, osend, orecv,
    l_sem, x_send, x_recv, w_send, w_recv, s_send, s_recv, p_send, p_recv,
    my_send, my_recv, mc_send, mc_recv, mf_send, mf_recv, o_send, o_recv,
):
    rows, width = x_hbm.shape
    quarter = wbuf.shape[3]
    heads_here = quarter // HEAD_DIM
    features = width * row_count
    per_half = rows // chunk

    row = lax.axis_index("row")
    col = lax.axis_index("col")
    y, c = row // 2, row % 2
    pair = {"row": 2 * y + (1 - c)}
    ypeer = {"row": 2 * (1 - y) + c}
    xpeer = {"col": 1 - col}

    def span(y_of, c_of):
        return pl.ds(pl.multiple_of((2 * y_of + c_of) * quarter, quarter), quarter)

    def remote(src, dst, send, recv, device):
        return pltpu.make_async_remote_copy(
            src_ref=src, dst_ref=dst, send_sem=send, recv_sem=recv,
            device_id=device, device_id_type=MESH)

    weights = (k_hbm, v_hbm, q_hbm)
    y_of = (1 - y, y)

    local = [
        pltpu.make_async_copy(x_hbm, xraw.at[0, 0], l_sem.at[0]),
        pltpu.make_async_copy(gain_hbm, gains.at[0], l_sem.at[1]),
    ]
    w_local = {}
    for side in range(2):
        for t in range(3):
            w_local[side, t] = pltpu.make_async_copy(
                weights[t].at[:, span(y_of[side], c)],
                wbuf.at[side, t, pl.ds(0, width)], l_sem.at[3 + side * 3 + t])
    wo_local = pltpu.make_async_copy(o_hbm, wo, l_sem.at[2])
    for copy in local:
        copy.start()
    for copy in w_local.values():
        copy.start()
    wo_local.start()

    barrier = pltpu.get_barrier_semaphore()
    for device in (pair, ypeer, xpeer):
        pl.semaphore_signal(barrier, inc=1, device_id=device, device_id_type=MESH)
    pl.semaphore_wait(barrier, 3)

    x_to_x = remote(x_hbm, xraw.at[1, 0], x_send.at[0], x_recv.at[0], xpeer)
    x_to_pair = remote(x_hbm, xraw.at[0, 1], x_send.at[1], x_recv.at[1], pair)
    g_to_pair = remote(gain_hbm, gains.at[1], x_send.at[2], x_recv.at[2], pair)
    x_forward = remote(xraw.at[1, 0], xraw.at[1, 1], x_send.at[3], x_recv.at[3], pair)
    w_pair = {}
    for side in range(2):
        for t in range(3):
            w_pair[side, t] = remote(
                weights[t].at[:, span(y_of[side], 1 - c)],
                wbuf.at[side, t, pl.ds(width, width)],
                w_send.at[side * 3 + t], w_recv.at[side * 3 + t], pair)
    x_to_x.start()
    g_to_pair.start()
    x_to_pair.start()
    for side in range(2):
        for t in range(3):
            w_pair[side, t].start()

    def prepare(half, part):
        gain = gains[part]

        @pl.loop(0, per_half)
        def _(j):
            at = pl.ds(pl.multiple_of(j * chunk, chunk), chunk)
            wide = xraw[half, part, at, :].astype(F32)
            total = jnp.broadcast_to(
                jnp.sum(wide * wide, axis=1, keepdims=True), (chunk, 128))
            if part == 0:
                ssq[half, at, :] = total
            else:
                ssq[half, at, :] += total
            xg[half, at, pl.ds(part * width, width)] = (wide * gain).astype(BF16)

    def squares(half):
        return remote(ssq_out.at[half], ssq_in.at[half], s_send.at[half], s_recv.at[half], ypeer)

    def send_squares(half):
        ssq_out[half] = jnp.transpose(ssq[half])[0:8, :]
        squares(half).start()

    def partial(half, t):
        return remote(psend.at[half, t], precv.at[half, t],
                      p_send.at[half, t], p_recv.at[half, t], ypeer)

    def product(half, side, t):
        return jnp.dot(xg[half], wbuf[side, t], preferred_element_type=F32)

    def away(half, t):
        psend[half, t] = product(half, 0, t).astype(BF16)
        partial(half, t).start()

    def home(half, t):
        pown[half, t] = product(half, 1, t)

    for copy in local:
        copy.wait()
    prepare(0, 0)
    g_to_pair.wait_recv()
    x_to_pair.wait_recv()
    prepare(0, 1)
    for t in range(2):
        w_local[0, t].wait()
        w_pair[0, t].wait_recv()
        away(0, t)
    send_squares(0)
    for t in range(3):
        w_local[1, t].wait()
        w_pair[1, t].wait_recv()
    w_local[0, QUERY].wait()
    w_pair[0, QUERY].wait_recv()

    @pl.loop(0, 3)
    def _(t):
        home(0, t)

    x_to_x.wait_recv()
    x_forward.start()
    prepare(1, 0)
    x_forward.wait_recv()
    prepare(1, 1)

    @pl.loop(0, 3)
    def _(t):
        away(1, t)

    away(0, QUERY)
    send_squares(1)

    @pl.loop(0, 3)
    def _(t):
        home(1, t)

    for half in range(2):
        squares(half).wait_recv()
        arrived = jnp.transpose(jnp.broadcast_to(ssq_in[half, 0:1, :], (128, rows)))
        scale[half] = lax.rsqrt((ssq[half] + arrived) / features + EPS)

    to_exponent = math.log2(math.e) / math.sqrt(HEAD_DIM)

    def combine(half, t):
        partial(half, t).wait_recv()
        factor = scale[half]
        if t == QUERY:
            factor = factor * to_exponent
        for h in range(heads_here):
            lanes = pl.ds(h * HEAD_DIM, HEAD_DIM)
            added = pown[half, t, :, lanes] + precv[half, t, :, lanes].astype(F32)
            qkv[t, pl.ds(half * rows, rows), lanes] = (added * factor).astype(BF16)

    def mixed(half, j, y_at, c_at):
        return mix.at[half, pl.ds(pl.multiple_of(j * chunk, chunk), chunk), span(y_at, c_at)]

    def mixed_y(half, j):
        block = mixed(half, j, y, c)
        return remote(block, block, my_send.at[half, j], my_recv.at[half, j], ypeer)

    def mixed_pair(half, j):
        block = mixed(half, j, y, c)
        return remote(block, block, mc_send.at[half, j], mc_recv.at[half, j], pair)

    def mixed_forward(half, j):
        block = mixed(half, j, 1 - y, c)
        return remote(block, block, mf_send.at[half, j], mf_recv.at[half, j], pair)

    def attend(half):
        @pl.loop(0, per_half)
        def _(j):
            at = pl.ds(pl.multiple_of(half * rows + j * chunk, chunk), chunk)
            parts = []
            for h in range(heads_here):
                lanes = pl.ds(h * HEAD_DIM, HEAD_DIM)
                scores = lax.dot_general(
                    qkv[QUERY, at, lanes], qkv[KEY, :, lanes],
                    (((1,), (1,)), ((), ())), preferred_element_type=F32)
                peak = jnp.max(scores, axis=1, keepdims=True)
                weight = jnp.exp2(scores - peak)
                denom = jnp.sum(weight, axis=1, keepdims=True)
                acc = jnp.dot(weight.astype(BF16), qkv[VALUE, :, lanes],
                              preferred_element_type=F32)
                parts.append((acc / denom).astype(BF16))
            mix[half, pl.ds(pl.multiple_of(j * chunk, chunk), chunk), span(y, c)] = (
                jnp.concatenate(parts, axis=1))
            mixed_y(half, j).start()
            mixed_pair(half, j).start()

    for half in range(2):
        for t in (KEY, VALUE):
            combine(half, t)
    for half in (1, 0):
        combine(half, QUERY)
        attend(half)

    wo_local.wait()

    def out_copy(j):
        return remote(osend.at[j], orecv.at[j], o_send.at[j], o_recv.at[j], xpeer)

    for half in (1, 0):
        @pl.loop(0, per_half)
        def _(j):
            mixed_y(half, j).wait_recv()
            mixed_forward(half, j).start()

        @pl.loop(0, per_half)
        def _(j):
            mixed_pair(half, j).wait_recv()
            mixed_forward(half, j).wait_recv()
            at = pl.ds(pl.multiple_of(j * chunk, chunk), chunk)
            terms = jnp.dot(mix[half, at, :], wo[...], preferred_element_type=F32)
            if half == 1:
                osend[j] = terms.astype(BF16)
                out_copy(j).start()
            else:
                out_copy(j).wait_recv()
                out_ref[at, :] = (terms + orecv[j].astype(F32)).astype(BF16)

    for copy in (x_to_x, x_to_pair, g_to_pair, x_forward):
        copy.wait_send()
    for copy in w_pair.values():
        copy.wait_send()
    for half in range(2):
        squares(half).wait_send()
        for t in range(3):
            partial(half, t).wait_send()
        for j in range(per_half):
            mixed_y(half, j).wait_send()
            mixed_pair(half, j).wait_send()
            mixed_forward(half, j).wait_send()
    for j in range(per_half):
        out_copy(j).wait_send()


def per_device(latents, norm_gain, q_weight, k_weight, v_weight, out_weight):
    row_count = lax.axis_size("row")
    assert row_count == 4 and lax.axis_size("col") == 2
    rows, width = latents.shape
    quarter = q_weight.shape[1] // row_count
    held = out_weight.shape[0]
    out_width = out_weight.shape[1]
    chunk = rows // 2
    per_half = rows // chunk
    dma = pltpu.SemaphoreType.DMA
    vmem = pltpu.VMEM
    scratch = [
        vmem((2, 2, rows, width), BF16),
        vmem((2, 1, width), F32),
        vmem((2, 3, 2 * width, quarter), BF16),
        vmem((held, out_width), BF16),
        vmem((2, rows, 2 * width), BF16),
        vmem((2, rows, 128), F32),
        vmem((2, 8, rows), F32),
        vmem((2, 8, rows), F32),
        vmem((2, rows, 128), F32),
        vmem((2, 3, rows, quarter), BF16),
        vmem((2, 3, rows, quarter), BF16),
        vmem((2, 3, rows, quarter), F32),
        vmem((3, 2 * rows, quarter), BF16),
        vmem((2, rows, held), BF16),
        vmem((per_half, chunk, out_width), BF16),
        vmem((per_half, chunk, out_width), BF16),
        dma((9,)),
        dma((4,)), dma((4,)),
        dma((6,)), dma((6,)),
        dma((2,)), dma((2,)),
        dma((2, 3)), dma((2, 3)),
    ] + [dma((2, per_half))] * 6 + [dma((per_half,))] * 2
    return pl.pallas_call(
        functools.partial(kernel, row_count, chunk),
        out_shape=jax.ShapeDtypeStruct((rows, out_width), BF16),
        in_specs=[pl.BlockSpec(memory_space=pl.ANY)] * 6,
        out_specs=pl.BlockSpec(memory_space=pltpu.VMEM),
        scratch_shapes=scratch,
        compiler_params=pltpu.CompilerParams(
            collective_id=0, has_side_effects=True, vmem_limit_bytes=60 * 1024 * 1024),
    )(latents, norm_gain.reshape(1, width), k_weight, v_weight, q_weight, out_weight)


def solution(mesh):
    return jax.shard_map(
        per_device,
        mesh=mesh,
        in_specs=(
            P(("dp", "col"), "row"),
            P(("dp", "row")),
            P(("dp", "row"), "col"),
            P(("dp", "row"), "col"),
            P(("dp", "row"), "col"),
            P(("dp", "col"), "row"),
        ),
        out_specs=P(("dp", "col"), "row"),
        check_vma=False,
    )
```

```python
import functools
import math

import jax
import jax.numpy as jnp
from jax import lax
from jax.experimental import pallas as pl
from jax.experimental.pallas import tpu as pltpu
from jax.sharding import PartitionSpec as P

HEAD_DIM = 128
EPS = 1e-06
MESH = pl.DeviceIdType.MESH
F32 = jnp.float32
BF16 = jnp.bfloat16
KEY, VALUE, QUERY = 0, 1, 2


def kernel(
    row_count, chunk,
    x_hbm, gain_hbm, k_hbm, v_hbm, q_hbm, o_hbm, out_ref,
    xraw, gains, wbuf, wo, xg, ssq, ssq_out, ssq_in, scale, psend, precv, pown,
    qkv, mix, osend, orecv, oown,
    l_sem, g_send, g_recv, x_send, x_recv, w_send, w_recv, s_send, s_recv,
    p_send, p_recv, m_send, m_recv, o_send, o_recv,
):
    rows, width = x_hbm.shape
    quarter = wbuf.shape[3]
    heads_here = quarter // HEAD_DIM
    features = width * row_count
    per_half = rows // chunk

    row = lax.axis_index("row")
    col = lax.axis_index("col")
    y, c = row // 2, row % 2
    pair = {"row": 2 * y + (1 - c)}
    ypeer = {"row": 2 * (1 - y) + c}
    xpeer = {"col": 1 - col}

    def span(y_of, c_of):
        return pl.ds(pl.multiple_of((2 * y_of + c_of) * quarter, quarter), quarter)

    def remote(src, dst, send, recv, device):
        return pltpu.make_async_remote_copy(
            src_ref=src, dst_ref=dst, send_sem=send, recv_sem=recv,
            device_id=device, device_id_type=MESH)

    weights = (k_hbm, v_hbm, q_hbm)
    y_of = (1 - y, y)

    def rows_of(g):
        return pl.ds(pl.multiple_of(g * chunk, chunk), chunk)

    x_local = [
        pltpu.make_async_copy(x_hbm.at[rows_of(g)], xraw.at[g, 0], l_sem.at[8 + g])
        for g in range(per_half)
    ]
    g_local = pltpu.make_async_copy(gain_hbm, gains.at[0], l_sem.at[0])
    w_local = {}
    for side in range(2):
        for t in range(3):
            w_local[side, t] = pltpu.make_async_copy(
                weights[t].at[:, span(y_of[side], c)],
                wbuf.at[side, t, pl.ds(0, width)], l_sem.at[2 + side * 3 + t])
    wo_local = pltpu.make_async_copy(o_hbm, wo, l_sem.at[1])
    g_local.start()
    for copy in x_local:
        copy.start()
    for copy in w_local.values():
        copy.start()
    wo_local.start()

    barrier = pltpu.get_barrier_semaphore()
    for device in (pair, ypeer, xpeer):
        pl.semaphore_signal(barrier, inc=1, device_id=device, device_id_type=MESH)
    pl.semaphore_wait(barrier, 3)

    g_to_pair = remote(gain_hbm, gains.at[1], g_send.at[0], g_recv.at[0], pair)
    x_to_x, x_to_pair, x_forward = [], [], []
    for g in range(per_half):
        x_to_pair.append(remote(
            x_hbm.at[rows_of(g)], xraw.at[g, 1], x_send.at[0, g], x_recv.at[0, g], pair))
        x_to_x.append(remote(
            x_hbm.at[rows_of(g)], xraw.at[per_half + g, 0],
            x_send.at[1, g], x_recv.at[1, g], xpeer))
        x_forward.append(remote(
            xraw.at[per_half + g, 0], xraw.at[per_half + g, 1],
            x_send.at[2, g], x_recv.at[2, g], pair))
    w_pair = {}
    for side in range(2):
        for t in range(3):
            w_pair[side, t] = remote(
                weights[t].at[:, span(y_of[side], 1 - c)],
                wbuf.at[side, t, pl.ds(width, width)],
                w_send.at[side * 3 + t], w_recv.at[side * 3 + t], pair)
    g_to_pair.start()
    for copy in x_to_pair:
        copy.start()
    for copy in x_to_x:
        copy.start()
    for side in range(2):
        for t in range(3):
            w_pair[side, t].start()

    def prepare(g, part):
        wide = xraw[g, part].astype(F32)
        total = jnp.broadcast_to(jnp.sum(wide * wide, axis=1, keepdims=True), (chunk, 128))
        if part == 0:
            ssq[g] = total
        else:
            ssq[g] += total
        xg[g, :, pl.ds(part * width, width)] = (wide * gains[part]).astype(BF16)

    def squares(g):
        return remote(ssq_out.at[g], ssq_in.at[g], s_send.at[g], s_recv.at[g], ypeer)

    def send_squares(g):
        ssq_out[g] = jnp.transpose(ssq[g])[0:8, :]
        squares(g).start()

    def partial(g, t):
        return remote(psend.at[g, t], precv.at[g, t], p_send.at[g, t], p_recv.at[g, t], ypeer)

    def product(g, side, t):
        return jnp.dot(xg[g], wbuf[side, t], preferred_element_type=F32)

    def away(g, t):
        psend[g, t] = product(g, 0, t).astype(BF16)
        partial(g, t).start()

    def home(first):
        @pl.loop(0, per_half)
        def _(g):
            @pl.loop(0, 3)
            def _(t):
                pown[first + g, t] = product(first + g, 1, t)

    near = range(per_half)
    far = range(per_half, 2 * per_half)

    g_local.wait()
    for g in near:
        x_local[g].wait()
        prepare(g, 0)
        if g == 0:
            g_to_pair.wait_recv()
        x_to_pair[g].wait_recv()
        prepare(g, 1)
        if g == 0:
            w_local[0, KEY].wait()
            w_pair[0, KEY].wait_recv()
        away(g, KEY)
    w_local[0, VALUE].wait()
    w_pair[0, VALUE].wait_recv()
    for g in near:
        away(g, VALUE)
        send_squares(g)
    for t in range(3):
        w_local[1, t].wait()
        w_pair[1, t].wait_recv()
    home(0)
    w_local[0, QUERY].wait()
    w_pair[0, QUERY].wait_recv()

    for g in far:
        x_to_x[g - per_half].wait_recv()
        x_forward[g - per_half].start()
        prepare(g, 0)
        x_forward[g - per_half].wait_recv()
        prepare(g, 1)
        for t in (KEY, VALUE):
            away(g, t)
        send_squares(g)
    for g in far:
        away(g, QUERY)
    away(0, QUERY)
    home(per_half)

    to_exponent = math.log2(math.e) / math.sqrt(HEAD_DIM)

    def combine(g, t):
        partial(g, t).wait_recv()
        factor = scale[g]
        if t == QUERY:
            factor = factor * to_exponent
        for h in range(heads_here):
            lanes = pl.ds(h * HEAD_DIM, HEAD_DIM)
            added = pown[g, t, :, lanes] + precv[g, t, :, lanes].astype(F32)
            qkv[t, rows_of(g), lanes] = (added * factor).astype(BF16)

    for g in (*near, *far):
        squares(g).wait_recv()
        arrived = jnp.transpose(jnp.broadcast_to(ssq_in[g, 0:1, :], (128, chunk)))
        scale[g] = lax.rsqrt((ssq[g] + arrived) / features + EPS)
        for t in (KEY, VALUE):
            combine(g, t)

    def mixed_y(g):
        block = mix.at[g, :, span(y, c)]
        return remote(block, block, m_send.at[0, g], m_recv.at[0, g], ypeer)

    def mixed_pair(g):
        block = mix.at[g, :, span(y, c)]
        return remote(block, block, m_send.at[1, g], m_recv.at[1, g], pair)

    def mixed_forward(g):
        block = mix.at[g, :, span(1 - y, c)]
        return remote(block, block, m_send.at[2, g], m_recv.at[2, g], pair)

    def attend(g):
        combine(g, QUERY)
        parts = []
        for h in range(heads_here):
            lanes = pl.ds(h * HEAD_DIM, HEAD_DIM)
            scores = lax.dot_general(
                qkv[QUERY, rows_of(g), lanes], qkv[KEY, :, lanes],
                (((1,), (1,)), ((), ())), preferred_element_type=F32)
            peak = jnp.max(scores, axis=1, keepdims=True)
            weight = jnp.exp2(scores - peak)
            denom = jnp.sum(weight, axis=1, keepdims=True)
            acc = jnp.dot(weight.astype(BF16), qkv[VALUE, :, lanes],
                          preferred_element_type=F32)
            parts.append((acc / denom).astype(BF16))
        mix[g, :, span(y, c)] = jnp.concatenate(parts, axis=1)
        mixed_y(g).start()
        mixed_pair(g).start()

    def forward(g):
        mixed_y(g).wait_recv()
        mixed_forward(g).start()

    def terms(g):
        mixed_pair(g).wait_recv()
        mixed_forward(g).wait_recv()
        return jnp.dot(mix[g], wo[...], preferred_element_type=F32)

    def out_copy(g):
        return remote(osend.at[g], orecv.at[g], o_send.at[g], o_recv.at[g], xpeer)

    def out_away(g):
        osend[g - per_half] = terms(g).astype(BF16)
        out_copy(g - per_half).start()

    for g in far:
        attend(g)
    for g in near[1:]:
        away(g, QUERY)
    attend(0)
    wo_local.wait()
    for g in far:
        forward(g)
        out_away(g)
    for g in near[1:]:
        attend(g)
    for g in near:
        forward(g)
        oown[g] = terms(g)
    for g in near:
        out_copy(g).wait_recv()
        out_ref[rows_of(g), :] = (oown[g] + orecv[g].astype(F32)).astype(BF16)

    g_to_pair.wait_send()
    for copy in (*x_to_x, *x_to_pair, *x_forward, *w_pair.values()):
        copy.wait_send()
    for g in (*near, *far):
        squares(g).wait_send()
        for t in range(3):
            partial(g, t).wait_send()
        mixed_y(g).wait_send()
        mixed_pair(g).wait_send()
        mixed_forward(g).wait_send()
    for g in near:
        out_copy(g).wait_send()


def per_device(latents, norm_gain, q_weight, k_weight, v_weight, out_weight):
    row_count = lax.axis_size("row")
    assert row_count == 4 and lax.axis_size("col") == 2
    rows, width = latents.shape
    quarter = q_weight.shape[1] // row_count
    held = out_weight.shape[0]
    out_width = out_weight.shape[1]
    chunk = rows // 2
    per_half = rows // chunk
    dma = pltpu.SemaphoreType.DMA
    vmem = pltpu.VMEM
    pieces = 2 * per_half
    scratch = [
        vmem((pieces, 2, chunk, width), BF16),
        vmem((2, 1, width), F32),
        vmem((2, 3, 2 * width, quarter), BF16),
        vmem((held, out_width), BF16),
        vmem((pieces, chunk, 2 * width), BF16),
        vmem((pieces, chunk, 128), F32),
        vmem((pieces, 8, chunk), F32),
        vmem((pieces, 8, chunk), F32),
        vmem((pieces, chunk, 128), F32),
        vmem((pieces, 3, chunk, quarter), BF16),
        vmem((pieces, 3, chunk, quarter), BF16),
        vmem((pieces, 3, chunk, quarter), F32),
        vmem((3, 2 * rows, quarter), BF16),
        vmem((pieces, chunk, held), BF16),
        vmem((per_half, chunk, out_width), BF16),
        vmem((per_half, chunk, out_width), BF16),
        vmem((per_half, chunk, out_width), F32),
        dma((8 + per_half,)),
        dma((1,)), dma((1,)),
        dma((3, per_half)), dma((3, per_half)),
        dma((6,)), dma((6,)),
        dma((pieces,)), dma((pieces,)),
        dma((pieces, 3)), dma((pieces, 3)),
        dma((3, pieces)), dma((3, pieces)),
        dma((per_half,)), dma((per_half,)),
    ]
    return pl.pallas_call(
        functools.partial(kernel, row_count, chunk),
        out_shape=jax.ShapeDtypeStruct((rows, out_width), BF16),
        in_specs=[pl.BlockSpec(memory_space=pl.ANY)] * 6,
        out_specs=pl.BlockSpec(memory_space=pltpu.VMEM),
        scratch_shapes=scratch,
        compiler_params=pltpu.CompilerParams(
            collective_id=0, has_side_effects=True, vmem_limit_bytes=60 * 1024 * 1024),
    )(latents, norm_gain.reshape(1, width), k_weight, v_weight, q_weight, out_weight)


def solution(mesh):
    return jax.shard_map(
        per_device,
        mesh=mesh,
        in_specs=(
            P(("dp", "col"), "row"),
            P(("dp", "row")),
            P(("dp", "row"), "col"),
            P(("dp", "row"), "col"),
            P(("dp", "row"), "col"),
            P(("dp", "col"), "row"),
        ),
        out_specs=P(("dp", "col"), "row"),
        check_vma=False,
    )
```

```python
import functools
import math

import jax
import jax.numpy as jnp
from jax import lax
from jax.experimental import pallas as pl
from jax.experimental.pallas import tpu as pltpu
from jax.sharding import PartitionSpec as P

HEAD_DIM = 128
EPS = 1e-06
MESH = pl.DeviceIdType.MESH
F32 = jnp.float32
BF16 = jnp.bfloat16
KEY, VALUE, QUERY = 0, 1, 2


def kernel(
    row_count, chunk,
    x_hbm, gain_hbm, k_hbm, v_hbm, q_hbm, o_hbm, out_ref,
    xraw, gains, wbuf, wo, xg, ssq, ssq_out, ssq_in, scale, psend, precv, pown,
    qkv, mix, osend, orecv, oown, oout,
    l_sem, g_send, g_recv, x_send, x_recv, w_send, w_recv, s_send, s_recv,
    p_send, p_recv, m_send, m_recv, o_send, o_recv,
):
    rows, width = x_hbm.shape
    quarter = wbuf.shape[3]
    heads_here = quarter // HEAD_DIM
    features = width * row_count
    per_half = rows // chunk

    row = lax.axis_index("row")
    col = lax.axis_index("col")
    y, c = row // 2, row % 2
    pair = {"row": 2 * y + (1 - c)}
    ypeer = {"row": 2 * (1 - y) + c}
    xpeer = {"col": 1 - col}

    def span(y_of, c_of):
        return pl.ds(pl.multiple_of((2 * y_of + c_of) * quarter, quarter), quarter)

    def remote(src, dst, send, recv, device):
        return pltpu.make_async_remote_copy(
            src_ref=src, dst_ref=dst, send_sem=send, recv_sem=recv,
            device_id=device, device_id_type=MESH)

    weights = (k_hbm, v_hbm, q_hbm)
    y_of = (1 - y, y)

    def rows_of(g):
        return pl.ds(pl.multiple_of(g * chunk, chunk), chunk)

    x_local = [
        pltpu.make_async_copy(x_hbm.at[rows_of(g)], xraw.at[g, 0], l_sem.at[8 + g])
        for g in range(per_half)
    ]
    g_local = pltpu.make_async_copy(gain_hbm, gains.at[0], l_sem.at[0])
    w_local = {}
    for side in range(2):
        for t in range(3):
            w_local[side, t] = pltpu.make_async_copy(
                weights[t].at[:, span(y_of[side], c)],
                wbuf.at[side, t, pl.ds(0, width)], l_sem.at[2 + side * 3 + t])
    wo_local = pltpu.make_async_copy(o_hbm, wo, l_sem.at[1])
    g_local.start()
    for copy in x_local:
        copy.start()
    for copy in w_local.values():
        copy.start()
    wo_local.start()

    barrier = pltpu.get_barrier_semaphore()
    for device in (pair, ypeer, xpeer):
        pl.semaphore_signal(barrier, inc=1, device_id=device, device_id_type=MESH)
    pl.semaphore_wait(barrier, 3)

    g_to_pair = remote(gain_hbm, gains.at[1], g_send.at[0], g_recv.at[0], pair)
    x_to_x, x_to_pair, x_forward = [], [], []
    for g in range(per_half):
        x_to_pair.append(remote(
            x_hbm.at[rows_of(g)], xraw.at[g, 1], x_send.at[0, g], x_recv.at[0, g], pair))
        x_to_x.append(remote(
            x_hbm.at[rows_of(g)], xraw.at[per_half + g, 0],
            x_send.at[1, g], x_recv.at[1, g], xpeer))
        x_forward.append(remote(
            xraw.at[per_half + g, 0], xraw.at[per_half + g, 1],
            x_send.at[2, g], x_recv.at[2, g], pair))
    w_pair = {}
    for side in range(2):
        for t in range(3):
            w_pair[side, t] = remote(
                weights[t].at[:, span(y_of[side], 1 - c)],
                wbuf.at[side, t, pl.ds(width, width)],
                w_send.at[side * 3 + t], w_recv.at[side * 3 + t], pair)
    x_to_pair[0].start()
    g_to_pair.start()
    w_pair[0, KEY].start()
    for copy in (*x_to_x, *x_to_pair[1:]):
        copy.start()
    for copy in list(w_pair.values())[1:]:
        copy.start()

    def prepare(g, part):
        wide = xraw[g, part].astype(F32)
        total = jnp.broadcast_to(jnp.sum(wide * wide, axis=1, keepdims=True), (chunk, 128))
        if part == 0:
            ssq[g] = total
        else:
            ssq[g] += total
        xg[g, :, pl.ds(part * width, width)] = (wide * gains[part]).astype(BF16)

    def squares(g):
        return remote(ssq_out.at[g], ssq_in.at[g], s_send.at[g], s_recv.at[g], ypeer)

    def send_squares(g):
        ssq_out[g] = jnp.transpose(ssq[g])[0:1, :]
        squares(g).start()

    def partial(g, t):
        return remote(psend.at[g, t], precv.at[g, t], p_send.at[g, t], p_recv.at[g, t], ypeer)

    def product(g, side, t):
        return jnp.dot(xg[g], wbuf[side, t], preferred_element_type=F32)

    def away(g, t):
        psend[g, t] = product(g, 0, t).astype(BF16)
        partial(g, t).start()

    def home(first):
        @pl.loop(0, per_half)
        def _(g):
            @pl.loop(0, 3)
            def _(t):
                pown[first + g, t] = product(first + g, 1, t)

    near = range(per_half)
    far = range(per_half, 2 * per_half)

    g_local.wait()
    for g in near:
        x_local[g].wait()
        prepare(g, 0)
    for g in near:
        if g == 0:
            g_to_pair.wait_recv()
        x_to_pair[g].wait_recv()
        prepare(g, 1)
        if g == 0:
            w_local[0, KEY].wait()
            w_pair[0, KEY].wait_recv()
        away(g, KEY)
    w_local[0, VALUE].wait()
    w_pair[0, VALUE].wait_recv()
    for g in near:
        away(g, VALUE)
        send_squares(g)
    for t in range(3):
        w_local[1, t].wait()
        w_pair[1, t].wait_recv()
    home(0)
    w_local[0, QUERY].wait()
    w_pair[0, QUERY].wait_recv()

    for g in far:
        x_to_x[g - per_half].wait_recv()
        x_forward[g - per_half].start()
        prepare(g, 0)
        x_forward[g - per_half].wait_recv()
        prepare(g, 1)
        for t in (KEY, VALUE):
            away(g, t)
        send_squares(g)
    for g in far:
        away(g, QUERY)
    home(per_half)

    to_exponent = math.log2(math.e) / math.sqrt(HEAD_DIM)

    def combine(g, t):
        partial(g, t).wait_recv()
        factor = scale[g]
        if t == QUERY:
            factor = factor * to_exponent
        for h in range(heads_here):
            lanes = pl.ds(h * HEAD_DIM, HEAD_DIM)
            added = pown[g, t, :, lanes] + precv[g, t, :, lanes].astype(F32)
            qkv[t, rows_of(g), lanes] = (added * factor).astype(BF16)

    for g in (*near, *far):
        squares(g).wait_recv()
        arrived = jnp.transpose(jnp.broadcast_to(ssq_in[g], (128, chunk)))
        scale[g] = lax.rsqrt((ssq[g] + arrived) / features + EPS)
        for t in (KEY, VALUE):
            combine(g, t)

    def mixed_y(g):
        block = mix.at[g, :, span(y, c)]
        return remote(block, block, m_send.at[0, g], m_recv.at[0, g], ypeer)

    def mixed_pair(g):
        block = mix.at[g, :, span(y, c)]
        return remote(block, block, m_send.at[1, g], m_recv.at[1, g], pair)

    def mixed_forward(g):
        block = mix.at[g, :, span(1 - y, c)]
        return remote(block, block, m_send.at[2, g], m_recv.at[2, g], pair)

    def attend(g):
        combine(g, QUERY)
        parts = []
        for h in range(heads_here):
            lanes = pl.ds(h * HEAD_DIM, HEAD_DIM)
            scores = lax.dot_general(
                qkv[QUERY, rows_of(g), lanes], qkv[KEY, :, lanes],
                (((1,), (1,)), ((), ())), preferred_element_type=F32)
            peak = jnp.max(scores, axis=1, keepdims=True)
            weight = jnp.exp2(scores - peak)
            denom = jnp.sum(weight, axis=1, keepdims=True)
            acc = jnp.dot(weight.astype(BF16), qkv[VALUE, :, lanes],
                          preferred_element_type=F32)
            parts.append((acc / denom).astype(BF16))
        mix[g, :, span(y, c)] = jnp.concatenate(parts, axis=1)
        mixed_y(g).start()
        mixed_pair(g).start()

    def chip_terms(g, y_at):
        held = pl.ds(pl.multiple_of(2 * y_at * quarter, 2 * quarter), 2 * quarter)
        return jnp.dot(mix[g, :, held], wo[held, :], preferred_element_type=F32)

    def terms(g):
        mixed_y(g).wait_recv()
        mixed_forward(g).start()
        mixed_pair(g).wait_recv()
        oown[g] = chip_terms(g, y)
        mixed_forward(g).wait_recv()
        return oown[g] + chip_terms(g, 1 - y)

    def out_copy(g):
        return remote(osend.at[g], orecv.at[g], o_send.at[g], o_recv.at[g], xpeer)

    def out_away(g):
        osend[g - per_half] = terms(g).astype(BF16)
        out_copy(g - per_half).start()

    for g in near:
        attend(per_half + g)
        away(g, QUERY)
    attend(0)
    wo_local.wait()
    for g in far:
        out_away(g)
    for g in near[1:]:
        attend(g)
    for g in near:
        oown[g] = terms(g)
    writes = []
    for g in near:
        out_copy(g).wait_recv()
        oout[g] = (oown[g] + orecv[g].astype(F32)).astype(BF16)
        writes.append(pltpu.make_async_copy(oout.at[g], out_ref.at[rows_of(g)], l_sem.at[g]))
        writes[-1].start()
    for copy in writes:
        copy.wait()

    g_to_pair.wait_send()
    for copy in (*x_to_x, *x_to_pair, *x_forward, *w_pair.values()):
        copy.wait_send()
    for g in (*near, *far):
        squares(g).wait_send()
        for t in range(3):
            partial(g, t).wait_send()
        mixed_y(g).wait_send()
        mixed_pair(g).wait_send()
        mixed_forward(g).wait_send()
    for g in near:
        out_copy(g).wait_send()


def per_device(latents, norm_gain, q_weight, k_weight, v_weight, out_weight):
    row_count = lax.axis_size("row")
    assert row_count == 4 and lax.axis_size("col") == 2
    rows, width = latents.shape
    quarter = q_weight.shape[1] // row_count
    held = out_weight.shape[0]
    out_width = out_weight.shape[1]
    chunk = rows // 2
    per_half = rows // chunk
    dma = pltpu.SemaphoreType.DMA
    vmem = pltpu.VMEM
    pieces = 2 * per_half
    scratch = [
        vmem((pieces, 2, chunk, width), BF16),
        vmem((2, 1, width), F32),
        vmem((2, 3, 2 * width, quarter), BF16),
        vmem((held, out_width), BF16),
        vmem((pieces, chunk, 2 * width), BF16),
        vmem((pieces, chunk, 128), F32),
        vmem((pieces, 1, chunk), F32),
        vmem((pieces, 1, chunk), F32),
        vmem((pieces, chunk, 128), F32),
        vmem((pieces, 3, chunk, quarter), BF16),
        vmem((pieces, 3, chunk, quarter), BF16),
        vmem((pieces, 3, chunk, quarter), F32),
        vmem((3, 2 * rows, quarter), BF16),
        vmem((pieces, chunk, held), BF16),
        vmem((per_half, chunk, out_width), BF16),
        vmem((per_half, chunk, out_width), BF16),
        vmem((pieces, chunk, out_width), F32),
        vmem((per_half, chunk, out_width), BF16),
        dma((8 + per_half,)),
        dma((1,)), dma((1,)),
        dma((3, per_half)), dma((3, per_half)),
        dma((6,)), dma((6,)),
        dma((pieces,)), dma((pieces,)),
        dma((pieces, 3)), dma((pieces, 3)),
        dma((3, pieces)), dma((3, pieces)),
        dma((per_half,)), dma((per_half,)),
    ]
    return pl.pallas_call(
        functools.partial(kernel, row_count, chunk),
        out_shape=jax.ShapeDtypeStruct((rows, out_width), BF16),
        in_specs=[pl.BlockSpec(memory_space=pltpu.HBM)] * 6,
        out_specs=pl.BlockSpec(memory_space=pl.ANY),
        scratch_shapes=scratch,
        compiler_params=pltpu.CompilerParams(
            collective_id=0, has_side_effects=True, vmem_limit_bytes=53 * 1024 * 1024),
    )(latents, norm_gain.reshape(1, width), k_weight, v_weight, q_weight, out_weight)


def solution(mesh):
    return jax.shard_map(
        per_device,
        mesh=mesh,
        in_specs=(
            P(("dp", "col"), "row"),
            P(("dp", "row")),
            P(("dp", "row"), "col"),
            P(("dp", "row"), "col"),
            P(("dp", "row"), "col"),
            P(("dp", "col"), "row"),
        ),
        out_specs=P(("dp", "col"), "row"),
        check_vma=False,
    )
```

```python
import functools
import math

import jax
import jax.numpy as jnp
from jax import lax
from jax.experimental import pallas as pl
from jax.experimental.pallas import tpu as pltpu
from jax.sharding import PartitionSpec as P

HEAD_DIM = 128
EPS = 1e-06
MESH = pl.DeviceIdType.MESH
F32 = jnp.float32
BF16 = jnp.bfloat16
KEY, VALUE, QUERY = 0, 1, 2


def kernel(
    row_count, chunk,
    x_hbm, gain_hbm, k_hbm, v_hbm, q_hbm, o_hbm, out_ref,
    xraw, gains, wbuf, wo, xg, ssq, ssq_out, ssq_in, scale, psend, precv, pown,
    qkv, mix, osend, orecv, oown, oout,
    l_sem, g_send, g_recv, x_send, x_recv, w_send, w_recv, s_send, s_recv,
    p_send, p_recv, m_send, m_recv, o_send, o_recv,
):
    rows, width = x_hbm.shape
    quarter = wbuf.shape[3]
    heads_here = quarter // HEAD_DIM
    features = width * row_count
    per_half = rows // chunk

    row = lax.axis_index("row")
    col = lax.axis_index("col")
    y, c = row // 2, row % 2
    pair = {"row": 2 * y + (1 - c)}
    ypeer = {"row": 2 * (1 - y) + c}
    xpeer = {"col": 1 - col}

    def span(y_of, c_of):
        return pl.ds(pl.multiple_of((2 * y_of + c_of) * quarter, quarter), quarter)

    def remote(src, dst, send, recv, device):
        return pltpu.make_async_remote_copy(
            src_ref=src, dst_ref=dst, send_sem=send, recv_sem=recv,
            device_id=device, device_id_type=MESH)

    weights = (k_hbm, v_hbm, q_hbm)
    y_of = (1 - y, y)

    def rows_of(g):
        return pl.ds(pl.multiple_of(g * chunk, chunk), chunk)

    x_local = [
        pltpu.make_async_copy(x_hbm.at[rows_of(g)], xraw.at[g, 0], l_sem.at[8 + g])
        for g in range(per_half)
    ]
    g_local = pltpu.make_async_copy(gain_hbm, gains.at[0], l_sem.at[0])
    w_local = {}
    for side in range(2):
        for t in range(3):
            w_local[side, t] = pltpu.make_async_copy(
                weights[t].at[:, span(y_of[side], c)],
                wbuf.at[side, t, pl.ds(0, width)], l_sem.at[2 + side * 3 + t])
    wo_local = pltpu.make_async_copy(o_hbm, wo, l_sem.at[1])
    g_local.start()
    for copy in x_local:
        copy.start()
    for copy in w_local.values():
        copy.start()
    wo_local.start()

    barrier = pltpu.get_barrier_semaphore()
    for device in (pair, ypeer, xpeer):
        pl.semaphore_signal(barrier, inc=1, device_id=device, device_id_type=MESH)
    pl.semaphore_wait(barrier, 3)

    g_to_pair = remote(gain_hbm, gains.at[1], g_send.at[0], g_recv.at[0], pair)
    x_to_x, x_to_pair, x_forward = [], [], []
    for g in range(per_half):
        x_to_pair.append(remote(
            x_hbm.at[rows_of(g)], xraw.at[g, 1], x_send.at[0, g], x_recv.at[0, g], pair))
        x_to_x.append(remote(
            x_hbm.at[rows_of(g)], xraw.at[per_half + g, 0],
            x_send.at[1, g], x_recv.at[1, g], xpeer))
        x_forward.append(remote(
            xraw.at[per_half + g, 0], xraw.at[per_half + g, 1],
            x_send.at[2, g], x_recv.at[2, g], pair))
    w_pair = {}
    for side in range(2):
        for t in range(3):
            w_pair[side, t] = remote(
                weights[t].at[:, span(y_of[side], 1 - c)],
                wbuf.at[side, t, pl.ds(width, width)],
                w_send.at[side * 3 + t], w_recv.at[side * 3 + t], pair)
    x_to_pair[0].start()
    g_to_pair.start()
    w_pair[0, KEY].start()
    for copy in (*x_to_x, *x_to_pair[1:]):
        copy.start()
    for copy in list(w_pair.values())[1:]:
        copy.start()

    def prepare(g, part):
        wide = xraw[g, part].astype(F32)
        total = jnp.broadcast_to(jnp.sum(wide * wide, axis=1, keepdims=True), (chunk, 128))
        if part == 0:
            ssq[g] = total
        else:
            ssq[g] += total
        xg[g, :, pl.ds(part * width, width)] = (wide * gains[part]).astype(BF16)

    def squares(g):
        return remote(ssq_out.at[g], ssq_in.at[g], s_send.at[g], s_recv.at[g], ypeer)

    def send_squares(g):
        ssq_out[g] = jnp.transpose(ssq[g])[0:1, :]
        squares(g).start()

    def partial(g, t):
        return remote(psend.at[g, t], precv.at[g, t], p_send.at[g, t], p_recv.at[g, t], ypeer)

    def product(g, side, t):
        return jnp.dot(xg[g], wbuf[side, t], preferred_element_type=F32)

    def away(g, t):
        psend[g, t] = product(g, 0, t).astype(BF16)
        partial(g, t).start()

    def home(first):
        @pl.loop(0, per_half)
        def _(g):
            @pl.loop(0, 3)
            def _(t):
                pown[first + g, t] = product(first + g, 1, t)

    near = range(per_half)
    far = range(per_half, 2 * per_half)

    g_local.wait()
    for g in near:
        x_local[g].wait()
        prepare(g, 0)
    for g in near:
        if g == 0:
            g_to_pair.wait_recv()
        x_to_pair[g].wait_recv()
        prepare(g, 1)
        if g == 0:
            w_local[0, KEY].wait()
            w_pair[0, KEY].wait_recv()
        away(g, KEY)
    w_local[0, VALUE].wait()
    w_pair[0, VALUE].wait_recv()
    for g in near:
        away(g, VALUE)
        send_squares(g)
    for t in range(3):
        w_local[1, t].wait()
        w_pair[1, t].wait_recv()
    home(0)
    w_local[0, QUERY].wait()
    w_pair[0, QUERY].wait_recv()

    for g in far:
        x_to_x[g - per_half].wait_recv()
        x_forward[g - per_half].start()
        prepare(g, 0)
        x_forward[g - per_half].wait_recv()
        prepare(g, 1)
        for t in (KEY, VALUE):
            away(g, t)
        send_squares(g)
    for g in far:
        away(g, QUERY)
    home(per_half)

    to_exponent = math.log2(math.e) / math.sqrt(HEAD_DIM)

    def combine(g, t):
        partial(g, t).wait_recv()
        factor = scale[g]
        if t == QUERY:
            factor = factor * to_exponent
        for h in range(heads_here):
            lanes = pl.ds(h * HEAD_DIM, HEAD_DIM)
            added = pown[g, t, :, lanes] + precv[g, t, :, lanes].astype(F32)
            qkv[t, rows_of(g), lanes] = (added * factor).astype(BF16)

    for g in (*near, *far):
        squares(g).wait_recv()
        arrived = jnp.transpose(jnp.broadcast_to(ssq_in[g], (128, chunk)))
        scale[g] = lax.rsqrt((ssq[g] + arrived) / features + EPS)
        for t in (KEY, VALUE):
            combine(g, t)

    def head_of(y_at, h):
        first = (2 * y_at + c) * quarter + h * HEAD_DIM
        return pl.ds(pl.multiple_of(first, HEAD_DIM), HEAD_DIM)

    def mixed_copy(kind, g, h, y_at, device):
        block = mix.at[g, :, head_of(y_at, h)]
        return remote(block, block, m_send.at[kind, g, h], m_recv.at[kind, g, h], device)

    def mixed_y(g, h):
        return mixed_copy(0, g, h, y, ypeer)

    def mixed_pair(g, h):
        return mixed_copy(1, g, h, y, pair)

    def mixed_forward(g, h):
        return mixed_copy(2, g, h, 1 - y, pair)

    def attend(g):
        combine(g, QUERY)
        for h in range(heads_here):
            lanes = pl.ds(h * HEAD_DIM, HEAD_DIM)
            scores = lax.dot_general(
                qkv[QUERY, rows_of(g), lanes], qkv[KEY, :, lanes],
                (((1,), (1,)), ((), ())), preferred_element_type=F32)
            peak = jnp.max(scores, axis=1, keepdims=True)
            weight = jnp.exp2(scores - peak)
            denom = jnp.sum(weight, axis=1, keepdims=True)
            acc = jnp.dot(weight.astype(BF16), qkv[VALUE, :, lanes],
                          preferred_element_type=F32)
            mix[g, :, head_of(y, h)] = (acc / denom).astype(BF16)
            mixed_y(g, h).start()
            mixed_pair(g, h).start()

    def chip_terms(g, y_at):
        held = pl.ds(pl.multiple_of(2 * y_at * quarter, 2 * quarter), 2 * quarter)
        return jnp.dot(mix[g, :, held], wo[held, :], preferred_element_type=F32)

    def terms(g):
        for h in range(heads_here):
            mixed_y(g, h).wait_recv()
            mixed_forward(g, h).start()
            mixed_pair(g, h).wait_recv()
        oown[g] = chip_terms(g, y)
        for h in range(heads_here):
            mixed_forward(g, h).wait_recv()
        return oown[g] + chip_terms(g, 1 - y)

    def out_copy(g):
        return remote(osend.at[g], orecv.at[g], o_send.at[g], o_recv.at[g], xpeer)

    def out_away(g):
        osend[g - per_half] = terms(g).astype(BF16)
        out_copy(g - per_half).start()

    for g in near:
        attend(per_half + g)
        away(g, QUERY)
    wo_local.wait()
    for g in near:
        out_away(per_half + g)
        attend(g)
    for g in near:
        oown[g] = terms(g)
    writes = []
    for g in near:
        out_copy(g).wait_recv()
        oout[g] = (oown[g] + orecv[g].astype(F32)).astype(BF16)
        writes.append(pltpu.make_async_copy(oout.at[g], out_ref.at[rows_of(g)], l_sem.at[g]))
        writes[-1].start()
    for copy in writes:
        copy.wait()

    g_to_pair.wait_send()
    for copy in (*x_to_x, *x_to_pair, *x_forward, *w_pair.values()):
        copy.wait_send()
    for g in (*near, *far):
        squares(g).wait_send()
        for t in range(3):
            partial(g, t).wait_send()
        for h in range(heads_here):
            mixed_y(g, h).wait_send()
            mixed_pair(g, h).wait_send()
            mixed_forward(g, h).wait_send()
    for g in near:
        out_copy(g).wait_send()


def per_device(latents, norm_gain, q_weight, k_weight, v_weight, out_weight):
    row_count = lax.axis_size("row")
    assert row_count == 4 and lax.axis_size("col") == 2
    rows, width = latents.shape
    quarter = q_weight.shape[1] // row_count
    held = out_weight.shape[0]
    out_width = out_weight.shape[1]
    chunk = rows // 2
    per_half = rows // chunk
    dma = pltpu.SemaphoreType.DMA
    vmem = pltpu.VMEM
    pieces = 2 * per_half
    scratch = [
        vmem((pieces, 2, chunk, width), BF16),
        vmem((2, 1, width), F32),
        vmem((2, 3, 2 * width, quarter), BF16),
        vmem((held, out_width), BF16),
        vmem((pieces, chunk, 2 * width), BF16),
        vmem((pieces, chunk, 128), F32),
        vmem((pieces, 1, chunk), F32),
        vmem((pieces, 1, chunk), F32),
        vmem((pieces, chunk, 128), F32),
        vmem((pieces, 3, chunk, quarter), BF16),
        vmem((pieces, 3, chunk, quarter), BF16),
        vmem((pieces, 3, chunk, quarter), F32),
        vmem((3, 2 * rows, quarter), BF16),
        vmem((pieces, chunk, held), BF16),
        vmem((per_half, chunk, out_width), BF16),
        vmem((per_half, chunk, out_width), BF16),
        vmem((pieces, chunk, out_width), F32),
        vmem((per_half, chunk, out_width), BF16),
        dma((8 + per_half,)),
        dma((1,)), dma((1,)),
        dma((3, per_half)), dma((3, per_half)),
        dma((6,)), dma((6,)),
        dma((pieces,)), dma((pieces,)),
        dma((pieces, 3)), dma((pieces, 3)),
        dma((3, pieces, quarter // HEAD_DIM)), dma((3, pieces, quarter // HEAD_DIM)),
        dma((per_half,)), dma((per_half,)),
    ]
    return pl.pallas_call(
        functools.partial(kernel, row_count, chunk),
        out_shape=jax.ShapeDtypeStruct((rows, out_width), BF16),
        in_specs=[pl.BlockSpec(memory_space=pltpu.HBM)] * 6,
        out_specs=pl.BlockSpec(memory_space=pl.ANY),
        scratch_shapes=scratch,
        compiler_params=pltpu.CompilerParams(
            collective_id=0, has_side_effects=True, vmem_limit_bytes=53 * 1024 * 1024),
    )(latents, pltpu.with_memory_space_constraint(norm_gain.reshape(1, width), pltpu.HBM), k_weight, v_weight, q_weight, out_weight)


def solution(mesh):
    return jax.shard_map(
        per_device,
        mesh=mesh,
        in_specs=(
            P(("dp", "col"), "row"),
            P(("dp", "row")),
            P(("dp", "row"), "col"),
            P(("dp", "row"), "col"),
            P(("dp", "row"), "col"),
            P(("dp", "col"), "row"),
        ),
        out_specs=P(("dp", "col"), "row"),
        check_vma=False,
    )
```

```python
import functools
import math

import jax
import jax.numpy as jnp
from jax import lax
from jax.experimental import pallas as pl
from jax.experimental.pallas import tpu as pltpu
from jax.sharding import PartitionSpec as P

HEAD_DIM = 128
EPS = 1e-06
MESH = pl.DeviceIdType.MESH
F32 = jnp.float32
BF16 = jnp.bfloat16
KEY, VALUE, QUERY = 0, 1, 2


def kernel(
    row_count, chunk,
    x_hbm, gain_hbm, k_hbm, v_hbm, q_hbm, o_hbm, out_ref,
    xraw, gains, wbuf, wo, xg, ssq, ssq_out, ssq_in, scale, psend, precv, pown,
    qkv, mix, osend, orecv, oown, oout,
    l_sem, g_send, g_recv, x_send, x_recv, w_send, w_recv, s_send, s_recv,
    p_send, p_recv, m_send, m_recv, o_send, o_recv,
):
    rows, width = x_hbm.shape
    quarter = wbuf.shape[3]
    heads_here = quarter // HEAD_DIM
    features = width * row_count
    per_half = rows // chunk

    row = lax.axis_index("row")
    col = lax.axis_index("col")
    y, c = row // 2, row % 2
    pair = {"row": 2 * y + (1 - c)}
    ypeer = {"row": 2 * (1 - y) + c}
    xpeer = {"col": 1 - col}

    def span(y_of, c_of):
        return pl.ds(pl.multiple_of((2 * y_of + c_of) * quarter, quarter), quarter)

    def remote(src, dst, send, recv, device):
        return pltpu.make_async_remote_copy(
            src_ref=src, dst_ref=dst, send_sem=send, recv_sem=recv,
            device_id=device, device_id_type=MESH)

    weights = (k_hbm, v_hbm, q_hbm)
    y_of = (1 - y, y)

    def rows_of(g):
        return pl.ds(pl.multiple_of(g * chunk, chunk), chunk)

    x_local = [
        pltpu.make_async_copy(x_hbm.at[rows_of(g)], xraw.at[g, 0], l_sem.at[8 + g])
        for g in range(per_half)
    ]
    g_local = pltpu.make_async_copy(gain_hbm, gains.at[0], l_sem.at[0])
    w_local = {}
    for side in range(2):
        for t in range(3):
            w_local[side, t] = pltpu.make_async_copy(
                weights[t].at[:, span(y_of[side], c)],
                wbuf.at[side, t, pl.ds(0, width)], l_sem.at[2 + side * 3 + t])
    wo_local = pltpu.make_async_copy(o_hbm, wo, l_sem.at[1])
    g_local.start()
    for copy in x_local:
        copy.start()
    for copy in w_local.values():
        copy.start()
    wo_local.start()

    barrier = pltpu.get_barrier_semaphore()
    for device in (pair, ypeer, xpeer):
        pl.semaphore_signal(barrier, inc=1, device_id=device, device_id_type=MESH)
    pl.semaphore_wait(barrier, 3)

    g_to_pair = remote(gain_hbm, gains.at[1], g_send.at[0], g_recv.at[0], pair)
    x_to_x, x_to_pair, x_forward = [], [], []
    for g in range(per_half):
        x_to_pair.append(remote(
            x_hbm.at[rows_of(g)], xraw.at[g, 1], x_send.at[0, g], x_recv.at[0, g], pair))
        x_to_x.append(remote(
            x_hbm.at[rows_of(g)], xraw.at[per_half + g, 0],
            x_send.at[1, g], x_recv.at[1, g], xpeer))
        x_forward.append(remote(
            xraw.at[per_half + g, 0], xraw.at[per_half + g, 1],
            x_send.at[2, g], x_recv.at[2, g], pair))
    w_pair = {}
    for side in range(2):
        for t in range(3):
            w_pair[side, t] = remote(
                weights[t].at[:, span(y_of[side], 1 - c)],
                wbuf.at[side, t, pl.ds(width, width)],
                w_send.at[side * 3 + t], w_recv.at[side * 3 + t], pair)
    x_to_pair[0].start()
    g_to_pair.start()
    w_pair[0, KEY].start()
    for copy in (*x_to_x, *x_to_pair[1:]):
        copy.start()
    for copy in list(w_pair.values())[1:]:
        copy.start()

    def prepare(g, part):
        wide = xraw[g, part].astype(F32)
        total = jnp.broadcast_to(jnp.sum(wide * wide, axis=1, keepdims=True), (chunk, 128))
        if part == 0:
            ssq[g] = total
        else:
            ssq[g] += total
        xg[g, :, pl.ds(part * width, width)] = (wide * gains[part]).astype(BF16)

    def squares(g):
        return remote(ssq_out.at[g], ssq_in.at[g], s_send.at[g], s_recv.at[g], ypeer)

    def send_squares(g):
        ssq_out[g] = jnp.transpose(ssq[g])[0:1, :]
        squares(g).start()

    def partial(g, t):
        return remote(psend.at[g, t], precv.at[g, t], p_send.at[g, t], p_recv.at[g, t], ypeer)

    def product(g, side, t):
        return jnp.dot(xg[g], wbuf[side, t], preferred_element_type=F32)

    def away(g, t):
        psend[g, t] = product(g, 0, t).astype(BF16)
        partial(g, t).start()

    def home(first):
        @pl.loop(0, per_half)
        def _(g):
            @pl.loop(0, 3)
            def _(t):
                pown[first + g, t] = product(first + g, 1, t)

    near = range(per_half)
    far = range(per_half, 2 * per_half)

    g_local.wait()
    for g in near:
        x_local[g].wait()
        prepare(g, 0)
    for g in near:
        if g == 0:
            g_to_pair.wait_recv()
        x_to_pair[g].wait_recv()
        prepare(g, 1)
        if g == 0:
            w_local[0, KEY].wait()
            w_pair[0, KEY].wait_recv()
        away(g, KEY)
    w_local[0, VALUE].wait()
    w_pair[0, VALUE].wait_recv()
    for g in near:
        away(g, VALUE)
        send_squares(g)
    for t in range(3):
        w_local[1, t].wait()
        w_pair[1, t].wait_recv()
    home(0)
    w_local[0, QUERY].wait()
    w_pair[0, QUERY].wait_recv()

    for g in far:
        x_to_x[g - per_half].wait_recv()
        x_forward[g - per_half].start()
        prepare(g, 0)
        x_forward[g - per_half].wait_recv()
        prepare(g, 1)
        for t in (KEY, VALUE):
            away(g, t)
        send_squares(g)
    for g in far:
        away(g, QUERY)
    home(per_half)

    to_exponent = math.log2(math.e) / math.sqrt(HEAD_DIM)

    def combine(g, t):
        partial(g, t).wait_recv()
        factor = scale[g]
        if t == QUERY:
            factor = factor * to_exponent
        for h in range(heads_here):
            lanes = pl.ds(h * HEAD_DIM, HEAD_DIM)
            added = pown[g, t, :, lanes] + precv[g, t, :, lanes].astype(F32)
            qkv[t, rows_of(g), lanes] = (added * factor).astype(BF16)

    for g in (*near, *far):
        squares(g).wait_recv()
        arrived = jnp.transpose(jnp.broadcast_to(ssq_in[g], (128, chunk)))
        scale[g] = lax.rsqrt((ssq[g] + arrived) / features + EPS)
        for t in (KEY, VALUE):
            combine(g, t)

    def head_of(y_at, h):
        first = (2 * y_at + c) * quarter + h * HEAD_DIM
        return pl.ds(pl.multiple_of(first, HEAD_DIM), HEAD_DIM)

    def mixed_copy(kind, g, h, y_at, device):
        block = mix.at[g, :, head_of(y_at, h)]
        return remote(block, block, m_send.at[kind, g, h], m_recv.at[kind, g, h], device)

    def mixed_y(g, h):
        return mixed_copy(0, g, h, y, ypeer)

    def mixed_pair(g, h):
        return mixed_copy(1, g, h, y, pair)

    def mixed_forward(g, h):
        return mixed_copy(2, g, h, 1 - y, pair)

    def attend(g):
        combine(g, QUERY)
        for h in range(heads_here):
            lanes = pl.ds(h * HEAD_DIM, HEAD_DIM)
            scores = lax.dot_general(
                qkv[QUERY, rows_of(g), lanes], qkv[KEY, :, lanes],
                (((1,), (1,)), ((), ())), preferred_element_type=F32)
            peak = jnp.max(scores, axis=1, keepdims=True)
            weight = jnp.exp2(scores - peak)
            denom = jnp.sum(weight, axis=1, keepdims=True)
            acc = jnp.dot(weight.astype(BF16), qkv[VALUE, :, lanes],
                          preferred_element_type=F32)
            mix[g, :, head_of(y, h)] = (acc / denom).astype(BF16)
            mixed_y(g, h).start()
            mixed_pair(g, h).start()

    def chip_terms(g, y_at):
        held = pl.ds(pl.multiple_of(2 * y_at * quarter, 2 * quarter), 2 * quarter)
        return jnp.dot(mix[g, :, held], wo[held, :], preferred_element_type=F32)

    def terms(g):
        for h in range(heads_here):
            mixed_y(g, h).wait_recv()
            mixed_forward(g, h).start()
            mixed_pair(g, h).wait_recv()
        oown[g] = chip_terms(g, y)
        for h in range(heads_here):
            mixed_forward(g, h).wait_recv()
        return oown[g] + chip_terms(g, 1 - y)

    def out_copy(g):
        return remote(osend.at[g], orecv.at[g], o_send.at[g], o_recv.at[g], xpeer)

    def out_away(g):
        osend[g - per_half] = terms(g).astype(BF16)
        out_copy(g - per_half).start()

    for g in near:
        attend(per_half + g)
        away(g, QUERY)
    wo_local.wait()
    for g in near:
        out_away(per_half + g)
        attend(g)
    writes = []
    for g in near:
        total = terms(g)
        out_copy(g).wait_recv()
        oout[g] = (total + orecv[g].astype(F32)).astype(BF16)
        writes.append(pltpu.make_async_copy(oout.at[g], out_ref.at[rows_of(g)], l_sem.at[g]))
        writes[-1].start()
    for copy in writes:
        copy.wait()

    g_to_pair.wait_send()
    for copy in (*x_to_x, *x_to_pair, *x_forward, *w_pair.values()):
        copy.wait_send()
    for g in (*near, *far):
        squares(g).wait_send()
        for t in range(3):
            partial(g, t).wait_send()
        for h in range(heads_here):
            mixed_y(g, h).wait_send()
            mixed_pair(g, h).wait_send()
            mixed_forward(g, h).wait_send()
    for g in near:
        out_copy(g).wait_send()


def per_device(latents, norm_gain, q_weight, k_weight, v_weight, out_weight):
    row_count = lax.axis_size("row")
    assert row_count == 4 and lax.axis_size("col") == 2
    rows, width = latents.shape
    quarter = q_weight.shape[1] // row_count
    held = out_weight.shape[0]
    out_width = out_weight.shape[1]
    chunk = rows // 2
    per_half = rows // chunk
    dma = pltpu.SemaphoreType.DMA
    vmem = pltpu.VMEM
    pieces = 2 * per_half
    scratch = [
        vmem((pieces, 2, chunk, width), BF16),
        vmem((2, 1, width), F32),
        vmem((2, 3, 2 * width, quarter), BF16),
        vmem((held, out_width), BF16),
        vmem((pieces, chunk, 2 * width), BF16),
        vmem((pieces, chunk, 128), F32),
        vmem((pieces, 1, chunk), F32),
        vmem((pieces, 1, chunk), F32),
        vmem((pieces, chunk, 128), F32),
        vmem((pieces, 3, chunk, quarter), BF16),
        vmem((pieces, 3, chunk, quarter), BF16),
        vmem((pieces, 3, chunk, quarter), F32),
        vmem((3, 2 * rows, quarter), BF16),
        vmem((pieces, chunk, held), BF16),
        vmem((per_half, chunk, out_width), BF16),
        vmem((per_half, chunk, out_width), BF16),
        vmem((pieces, chunk, out_width), F32),
        vmem((per_half, chunk, out_width), BF16),
        dma((8 + per_half,)),
        dma((1,)), dma((1,)),
        dma((3, per_half)), dma((3, per_half)),
        dma((6,)), dma((6,)),
        dma((pieces,)), dma((pieces,)),
        dma((pieces, 3)), dma((pieces, 3)),
        dma((3, pieces, quarter // HEAD_DIM)), dma((3, pieces, quarter // HEAD_DIM)),
        dma((per_half,)), dma((per_half,)),
    ]
    return pl.pallas_call(
        functools.partial(kernel, row_count, chunk),
        out_shape=jax.ShapeDtypeStruct((rows, out_width), BF16),
        in_specs=[pl.BlockSpec(memory_space=pltpu.HBM)] * 6,
        out_specs=pl.BlockSpec(memory_space=pl.ANY),
        scratch_shapes=scratch,
        compiler_params=pltpu.CompilerParams(
            collective_id=0, has_side_effects=True, vmem_limit_bytes=53 * 1024 * 1024),
    )(latents, pltpu.with_memory_space_constraint(norm_gain.reshape(1, width), pltpu.HBM), k_weight, v_weight, q_weight, out_weight)


def solution(mesh):
    return jax.shard_map(
        per_device,
        mesh=mesh,
        in_specs=(
            P(("dp", "col"), "row"),
            P(("dp", "row")),
            P(("dp", "row"), "col"),
            P(("dp", "row"), "col"),
            P(("dp", "row"), "col"),
            P(("dp", "col"), "row"),
        ),
        out_specs=P(("dp", "col"), "row"),
        check_vma=False,
    )
```
